32 devices in a mesh: grp: 1, row: 8 (over z, y), br: 2 (over core), pb: 2 (over x).
Axes of the slice: x: 2, y: 2, z: 4, core: 2. Of those that a mesh axis runs over, the one named last changes fastest.
Arguments:
- homolog_representation: bfloat16 [128, 64, 256], P(('grp', 'pb'), ('row', 'br')), may hold values from -6 to 6
- pair_state: bfloat16 [64, 64, 128], P(('grp', 'row', 'br'), 'pb'), may hold values from -6 to 6
- genuine_chain_indicator: int32 [128], P('grp'), may hold values from 0 to 1
- resolved_mask: int32 [64], P('grp'), may hold values from 0 to 1
- crop_positions: int32 [64], P('grp'), may hold values from 0 to 12799, as said below
- relative_position_table: bfloat16 [65, 128], replicated, may hold values from -6 to 6
- column_query_key_value_gate: bfloat16 [256, 1024], replicated, may hold values from -48 to 48
- vertical_attention_projector: bfloat16 [256, 256], replicated, may hold values from -1.5 to 1.5
- expansion_coefficients: bfloat16 [256, 1024], replicated, may hold values from -0.375 to 0.375
- contraction_coefficients: bfloat16 [1024, 256], replicated, may hold values from -0.1875 to 0.1875
- operand_duo_projector: bfloat16 [256, 64], replicated, may hold values from -0.375 to 0.375
- tensor_product_projector: bfloat16 [1024, 128], replicated, may hold values from -2 to 2
- triangle_query_key_value_gate: bfloat16 [128, 512], replicated, may hold values from -48 to 48
- triangle_bias_weight: bfloat16 [128, 4], replicated, may hold values from -0.5 to 0.5
- triangle_output_weight: bfloat16 [128, 128], replicated, may hold values from -2 to 2
- pair_up_weight: bfloat16 [128, 512], replicated, may hold values from -0.5 to 0.5
- pair_down_weight: bfloat16 [512, 128], replicated, may hold values from -0.25 to 0.25
Outputs:
- refreshed_homologs: bfloat16 [128, 64, 256], P(('grp', 'pb'), ('row', 'br'))
- pair_updated: bfloat16 [64, 64, 128], P(('grp', 'row', 'br'), 'pb')
The draws below stay inside these ranges and needn't reach their ends.
Inputs may be any that keep to these rules, and one draw needn't show every extreme that they name: `crop_positions`: strictly increasing; the last entry is exactly 12799.
All inputs are finite; a program needn't handle non-finite values.
Results may differ from the reference program's by a relative error of at most 0.012.
Values may be sent and summed in bfloat16 or wider, within the bound.
No kernel may reach another device: no remote copies, remote signals or barrier semaphores. Data moves between devices by JAX's collectives and lax.ppermute only.
A program may use at most 64 MiB of HBM per device.

```python
import math
import jax
import jax.numpy as jnp
from jax import lax

ALIGNED_FEATURES = 256
COUPLING_DEPTH = 128
VERTICAL_ATTENDS = 8
TRI_HEADS = 4
SUBSPACE_DEPTH = 32
OPERAND_FEATURES = 32
EXPANSION_NEURONS = 1024
PAIR_FF = 512
RELPOS_MAX = 32
CHAINS_PER_SHARD = 64
WINDOW_AMINOS = 64
ALIGNED_CHAINS = 128


def draw_genuine_chain_indicator(key, part):
    selections = jax.random.randint(key, (ALIGNED_CHAINS,), 0, 4)
    leading_index = jnp.arange(ALIGNED_CHAINS) == 0
    return jnp.where(leading_index, 1, (selections != 0).astype(jnp.int32)).astype(jnp.int32)


def draw_resolved_mask(key, part):
    selections = jax.random.randint(key, (WINDOW_AMINOS,), 0, 8)
    leading_index = jnp.arange(WINDOW_AMINOS) == 0
    return jnp.where(leading_index, 1, (selections != 0).astype(jnp.int32)).astype(jnp.int32)


def draw_crop_positions(key, part):
    key_break, key_jump = jax.random.split(key, 2)
    breaks = jax.random.randint(key_break, (WINDOW_AMINOS,), 0, 16) == 0
    jumps = jax.random.randint(key_jump, (WINDOW_AMINOS,), 2, 200)
    steps_between = jnp.where(breaks, jumps, 1)
    steps_between = jnp.where(jnp.arange(WINDOW_AMINOS) == 0, 0, steps_between).astype(jnp.int32)
    running = jnp.cumsum(steps_between).astype(jnp.int32)
    shift = WINDOW_AMINOS * 200 - 1 - running[WINDOW_AMINOS - 1]
    return (running + shift).astype(jnp.int32)


def paired_coefficients(key, width, heads):
    key_base = jax.random.fold_in(key, 0)
    base = jnp.clip(jax.random.normal(key_base, (width, 4, heads, SUBSPACE_DEPTH), jnp.float32), -6.0, 6.0) * width ** (-0.5)
    return base


def draw_column_query_key_value_gate(key, part):
    return paired_coefficients(key, ALIGNED_FEATURES, VERTICAL_ATTENDS).reshape(ALIGNED_FEATURES, 4 * ALIGNED_FEATURES).astype(jnp.bfloat16)


def draw_triangle_query_key_value_gate(key, part):
    drawn = paired_coefficients(key, COUPLING_DEPTH, TRI_HEADS)
    return jnp.transpose(drawn, (0, 2, 1, 3)).reshape(COUPLING_DEPTH, 4 * COUPLING_DEPTH).astype(jnp.bfloat16)


def block_levels(stream_key, shape, cuts, low, top_value):
    def one(dim, blocks):
        steps = jax.random.uniform(jax.random.fold_in(jax.random.fold_in(stream_key, 6), dim), (blocks,), jnp.float32, low / len(cuts), top_value / len(cuts))
        return jnp.repeat(jnp.exp(steps), shape[dim] // blocks).reshape((-1,) + (1,) * (len(shape) - dim - 1))

    loudness = one(*cuts[0])
    for cut in cuts[1:]:
        loudness = loudness * one(*cut)
    return loudness


def bell_draw(stream_key, dims, scale, reach, pieces=(), dtype=jnp.bfloat16):
    values = scale * jax.random.normal(stream_key, dims, jnp.float32)
    if pieces:
        values = values * block_levels(stream_key, dims, pieces, -0.22, 0.18)
    return jnp.clip(values, -reach, reach).astype(dtype)


def setup_inputs(seed: int = 0, part: int = 0) -> dict:
    keys = jax.random.split(jax.random.key(seed), 18)
    own_keys = jax.random.split(jax.random.fold_in(keys[17], part), 18)
    homolog_representation = bell_draw(own_keys[0], (ALIGNED_CHAINS, WINDOW_AMINOS, ALIGNED_FEATURES), 1.0, 6.0, ((0, 2), (1, 16)))
    pair_state = bell_draw(own_keys[1], (WINDOW_AMINOS, WINDOW_AMINOS, COUPLING_DEPTH), 1.0, 6.0, ((0, 16), (1, 2)))
    genuine_chain_indicator = draw_genuine_chain_indicator(jax.random.fold_in(jax.random.fold_in(keys[17], part), 71), part)
    resolved_mask = draw_resolved_mask(jax.random.fold_in(jax.random.fold_in(keys[17], part), 71), part)
    crop_positions = draw_crop_positions(jax.random.fold_in(jax.random.fold_in(keys[17], part), 71), part)
    relative_position_table = bell_draw(keys[5], (2 * RELPOS_MAX + 1, COUPLING_DEPTH), 1.0, 6.0)
    column_query_key_value_gate = draw_column_query_key_value_gate(jax.random.fold_in(keys[17], 71), part)
    vertical_attention_projector = bell_draw(keys[7], (ALIGNED_FEATURES, ALIGNED_FEATURES), (ALIGNED_FEATURES // 16) ** -0.5, 1.5)
    expansion_coefficients = bell_draw(keys[8], (ALIGNED_FEATURES, EXPANSION_NEURONS), ALIGNED_FEATURES ** -0.5, 0.375)
    contraction_coefficients = bell_draw(keys[9], (EXPANSION_NEURONS, ALIGNED_FEATURES), EXPANSION_NEURONS ** -0.5, 0.1875)
    operand_duo_projector = bell_draw(keys[10], (ALIGNED_FEATURES, 2 * OPERAND_FEATURES), ALIGNED_FEATURES ** -0.5, 0.375)
    tensor_product_projector = bell_draw(keys[11], (OPERAND_FEATURES * OPERAND_FEATURES, COUPLING_DEPTH), (max(1, OPERAND_FEATURES * OPERAND_FEATURES // ALIGNED_CHAINS)) ** -0.5, 2.0)
    triangle_query_key_value_gate = draw_triangle_query_key_value_gate(jax.random.fold_in(keys[17], 71), part)
    triangle_bias_weight = bell_draw(keys[13], (COUPLING_DEPTH, TRI_HEADS), COUPLING_DEPTH ** -0.5, 0.5)
    triangle_output_weight = bell_draw(keys[14], (COUPLING_DEPTH, COUPLING_DEPTH), (COUPLING_DEPTH // 16) ** -0.5, 2.0)
    pair_up_weight = bell_draw(keys[15], (COUPLING_DEPTH, PAIR_FF), COUPLING_DEPTH ** -0.5, 0.5)
    pair_down_weight = bell_draw(keys[16], (PAIR_FF, COUPLING_DEPTH), PAIR_FF ** -0.5, 0.25)
    return dict(homolog_representation=homolog_representation, pair_state=pair_state, genuine_chain_indicator=genuine_chain_indicator, resolved_mask=resolved_mask, crop_positions=crop_positions, relative_position_table=relative_position_table, column_query_key_value_gate=column_query_key_value_gate, vertical_attention_projector=vertical_attention_projector, expansion_coefficients=expansion_coefficients, contraction_coefficients=contraction_coefficients, operand_duo_projector=operand_duo_projector, tensor_product_projector=tensor_product_projector, triangle_query_key_value_gate=triangle_query_key_value_gate, triangle_bias_weight=triangle_bias_weight, triangle_output_weight=triangle_output_weight, pair_up_weight=pair_up_weight, pair_down_weight=pair_down_weight)


NORM_EPS = 1e-05
MASK_NEGATIVE = 1000000000.0

def layer_normalize(values):
    values = values.astype(jnp.float32)
    centre = lax.optimization_barrier(jnp.mean(values, axis=-1, keepdims=True))
    centred = values - centre
    spread = lax.optimization_barrier(jnp.mean(centred * centred, axis=-1, keepdims=True))
    return (centred * lax.rsqrt(spread + NORM_EPS)).astype(jnp.bfloat16)

def rounded_weights(exp_scores):
    return lax.optimization_barrier(exp_scores.astype(jnp.bfloat16)).astype(jnp.float32)

def reference(homolog_representation, pair_state, genuine_chain_indicator, resolved_mask, crop_positions, relative_position_table, column_query_key_value_gate, vertical_attention_projector, expansion_coefficients, contraction_coefficients, operand_duo_projector, tensor_product_projector, triangle_query_key_value_gate, triangle_bias_weight, triangle_output_weight, pair_up_weight, pair_down_weight):
    score_scale = SUBSPACE_DEPTH ** (-0.5)
    standardized_representation = layer_normalize(homolog_representation)
    reshaped_standardized = standardized_representation.reshape(ALIGNED_CHAINS * WINDOW_AMINOS, ALIGNED_FEATURES)
    linear_mapped_representation = jnp.dot(reshaped_standardized, column_query_key_value_gate, preferred_element_type=jnp.float32).astype(jnp.bfloat16)
    linear_mapped_representation = linear_mapped_representation.reshape(ALIGNED_CHAINS, WINDOW_AMINOS, 4, VERTICAL_ATTENDS, SUBSPACE_DEPTH)
    shard_residue_span = math.gcd(WINDOW_AMINOS, 16)
    residuewise_arrangement = jnp.transpose(linear_mapped_representation, (1, 0, 2, 3, 4)).reshape(WINDOW_AMINOS // shard_residue_span, shard_residue_span, ALIGNED_CHAINS, 4, VERTICAL_ATTENDS, SUBSPACE_DEPTH)
    sequence_bias = (genuine_chain_indicator.astype(jnp.float32) - 1.0) * MASK_NEGATIVE

    def column_attention(block):
        block = block.astype(jnp.float32)
        query_matrix_rows = block[:, :, 0]
        key_matrix_rows = block[:, :, 1]
        value_matrix_rows = block[:, :, 2]
        gate_values_rows = block[:, :, 3]
        scores = jnp.einsum('cshd,cthd->chst', query_matrix_rows, key_matrix_rows) * score_scale + sequence_bias
        soft_top = lax.optimization_barrier(jnp.max(scores, axis=-1, keepdims=True))
        exp_scores = jnp.exp(scores - soft_top)
        soft_total = lax.optimization_barrier(jnp.sum(exp_scores, axis=-1))
        weights = rounded_weights(exp_scores)
        mixed_out = jnp.einsum('chst,cthd->cshd', weights, value_matrix_rows) / jnp.transpose(soft_total, (0, 2, 1))[..., None]
        return (jax.nn.sigmoid(gate_values_rows) * mixed_out).astype(jnp.bfloat16)
    mixed_contributions = lax.map(column_attention, residuewise_arrangement)
    mixed_contributions = jnp.transpose(mixed_contributions.reshape(WINDOW_AMINOS, ALIGNED_CHAINS, ALIGNED_FEATURES), (1, 0, 2)).reshape(ALIGNED_CHAINS * WINDOW_AMINOS, ALIGNED_FEATURES)
    intermediate_representation = homolog_representation.astype(jnp.float32).reshape(ALIGNED_CHAINS * WINDOW_AMINOS, ALIGNED_FEATURES) + jnp.dot(mixed_contributions, vertical_attention_projector, preferred_element_type=jnp.float32)
    expanded_activation = jax.nn.relu(jnp.dot(layer_normalize(intermediate_representation), expansion_coefficients, preferred_element_type=jnp.float32)).astype(jnp.bfloat16)
    refreshed_homologs = (intermediate_representation + jnp.dot(expanded_activation, contraction_coefficients, preferred_element_type=jnp.float32)).astype(jnp.bfloat16).reshape(ALIGNED_CHAINS, WINDOW_AMINOS, ALIGNED_FEATURES)
    rel_bins = jnp.clip(crop_positions[:, None] - crop_positions[None, :], -RELPOS_MAX, RELPOS_MAX) + RELPOS_MAX
    pair_in = pair_state.astype(jnp.float32) + relative_position_table.astype(jnp.float32)[rel_bins]
    pair_norm = layer_normalize(pair_in).reshape(WINDOW_AMINOS * WINDOW_AMINOS, COUPLING_DEPTH)
    tri_proj = jnp.dot(pair_norm, triangle_query_key_value_gate, preferred_element_type=jnp.float32).astype(jnp.bfloat16)
    tri_proj = tri_proj.reshape(WINDOW_AMINOS, WINDOW_AMINOS, TRI_HEADS, 4, SUBSPACE_DEPTH)
    tri_bias = jnp.dot(pair_norm, triangle_bias_weight, preferred_element_type=jnp.float32).astype(jnp.bfloat16)
    key_mask = (resolved_mask.astype(jnp.float32) - 1.0) * MASK_NEGATIVE
    head_bias = jnp.transpose(tri_bias.reshape(WINDOW_AMINOS, WINDOW_AMINOS, TRI_HEADS), (2, 0, 1)).astype(jnp.float32) + key_mask
    chain_partitions = ALIGNED_CHAINS // CHAINS_PER_SHARD
    tensor_operand_entries = (jnp.dot(reshaped_standardized, operand_duo_projector, preferred_element_type=jnp.float32).reshape(ALIGNED_CHAINS, WINDOW_AMINOS, 2 * OPERAND_FEATURES) * genuine_chain_indicator.astype(jnp.float32)[:, None, None]).astype(jnp.bfloat16)
    left_groups = tensor_operand_entries[:, :, :OPERAND_FEATURES].reshape(chain_partitions, CHAINS_PER_SHARD, WINDOW_AMINOS, OPERAND_FEATURES)
    right_groups = tensor_operand_entries[:, :, OPERAND_FEATURES:].reshape(chain_partitions, CHAINS_PER_SHARD, WINDOW_AMINOS, OPERAND_FEATURES).astype(jnp.float32)
    sequence_total = jnp.sum(genuine_chain_indicator.astype(jnp.float32))
    block_rows = math.gcd(WINDOW_AMINOS, 8)
    proj_blocks = tri_proj.reshape(WINDOW_AMINOS // block_rows, block_rows, WINDOW_AMINOS, TRI_HEADS, 4, SUBSPACE_DEPTH)
    left_blocks = jnp.transpose(left_groups, (2, 0, 1, 3)).reshape(WINDOW_AMINOS // block_rows, block_rows, chain_partitions, CHAINS_PER_SHARD, OPERAND_FEATURES)

    def row_update(block):
        block_proj, block_left = block
        block_proj = block_proj.astype(jnp.float32)
        query_matrix_rows = block_proj[:, :, :, 0]
        key_matrix_rows = block_proj[:, :, :, 1]
        value_matrix_rows = block_proj[:, :, :, 2]
        gate_values_rows = block_proj[:, :, :, 3]
        scores = jnp.einsum('ijhd,ikhd->ihjk', query_matrix_rows, key_matrix_rows) * score_scale + head_bias
        soft_top = lax.optimization_barrier(jnp.max(scores, axis=-1, keepdims=True))
        exp_scores = jnp.exp(scores - soft_top)
        soft_total = lax.optimization_barrier(jnp.sum(exp_scores, axis=-1))
        weights = rounded_weights(exp_scores)
        mixed_out = jnp.einsum('ihjk,ikhd->ijhd', weights, value_matrix_rows) / jnp.transpose(soft_total, (0, 2, 1))[..., None]
        gated = (jax.nn.sigmoid(gate_values_rows) * mixed_out).astype(jnp.bfloat16).reshape(block_rows * WINDOW_AMINOS, COUPLING_DEPTH)
        tri_update = jnp.dot(gated, triangle_output_weight, preferred_element_type=jnp.float32).reshape(block_rows, WINDOW_AMINOS, COUPLING_DEPTH)
        outer_prod = jnp.einsum('igsc,gsje->gijce', block_left.astype(jnp.float32), right_groups).astype(jnp.bfloat16)
        projected = jnp.dot(outer_prod.reshape(chain_partitions * block_rows * WINDOW_AMINOS, OPERAND_FEATURES * OPERAND_FEATURES), tensor_product_projector, preferred_element_type=jnp.float32)
        opm_update = lax.optimization_barrier(jnp.sum(projected.reshape(chain_partitions, block_rows, WINDOW_AMINOS, COUPLING_DEPTH) / sequence_total, axis=0))
        return tri_update + opm_update
    update = lax.map(row_update, (proj_blocks, left_blocks)).reshape(WINDOW_AMINOS, WINDOW_AMINOS, COUPLING_DEPTH)
    pair_mid = (pair_in + update).reshape(WINDOW_AMINOS * WINDOW_AMINOS, COUPLING_DEPTH)
    pair_hidden = jax.nn.relu(jnp.dot(layer_normalize(pair_mid), pair_up_weight, preferred_element_type=jnp.float32)).astype(jnp.bfloat16)
    pair_updated = (pair_mid + jnp.dot(pair_hidden, pair_down_weight, preferred_element_type=jnp.float32)).astype(jnp.bfloat16).reshape(WINDOW_AMINOS, WINDOW_AMINOS, COUPLING_DEPTH)
    return (refreshed_homologs, pair_updated)
```

```python
import functools

import jax
import jax.numpy as jnp
from jax import lax
from jax.experimental import pallas as pl
from jax.experimental.pallas import tpu as pltpu
from jax.sharding import PartitionSpec as P

VERTICAL_ATTENDS = 8
TRI_HEADS = 4
SUBSPACE_DEPTH = 32
RELPOS_MAX = 32
NORM_EPS = 1e-05
MASK_NEGATIVE = 1000000000.0
LANES = 128
F32 = jnp.float32
BF16 = jnp.bfloat16


def normalize(values):
    centre = jnp.mean(values, axis=-1, keepdims=True)
    centred = values - centre
    spread = jnp.mean(centred * centred, axis=-1, keepdims=True)
    return (centred * lax.rsqrt(spread + NORM_EPS)).astype(BF16)


def dot(a, b):
    return jnp.dot(a, b, preferred_element_type=F32)


def dot_t(a, b):
    return lax.dot_general(a, b, (((1,), (1,)), ((), ())), preferred_element_type=F32)


def residue_rows(scratch, residue, seqs, rows, blocks):
    step = rows * blocks
    parts = [scratch[pl.ds(b * rows + residue, seqs, stride=step), :] for b in range(blocks)]
    return jnp.concatenate(parts, axis=1)


def roll_left(row, amount):
    n = row.shape[1]
    wide = jnp.broadcast_to(row, (8, n))
    return pltpu.roll(wide, lax.rem(n - amount, n), 1)


def call(body, out_shape, args, smem=(), scratch=(), flops=10**8, name=None):
    specs = [
        pl.BlockSpec(memory_space=pltpu.SMEM if n in smem else pltpu.VMEM)
        for n in range(len(args))
    ]
    outs = jax.tree.map(lambda _: pl.BlockSpec(memory_space=pltpu.VMEM), out_shape)
    return pl.pallas_call(
        body,
        out_shape=out_shape,
        in_specs=specs,
        out_specs=outs,
        scratch_shapes=list(scratch),
        name=name,
        compiler_params=pltpu.CompilerParams(vmem_limit_bytes=28 << 20),
        cost_estimate=pl.CostEstimate(flops=flops, bytes_accessed=1 << 20, transcendentals=0),
    )(*args)


def local_kernel(
    dims, h_ref, wqkvg_ref, wopt_ref, wtp_ref, gen_ref,
    qkvg_ref, part_ref, lw_ref, hs, wf,
):
    seqs, rows, blocks, outer = dims
    p = lax.axis_index("pb")
    hs[...] = h_ref[...].astype(F32)
    wf[...] = wtp_ref[...].astype(F32)
    norm = jnp.concatenate(
        [normalize(residue_rows(hs, r, seqs, rows, blocks)) for r in range(rows)], axis=0
    )
    mask = roll_left(gen_ref[...].astype(F32), p * seqs)[:1, :seqs]
    fold = LANES // seqs
    groups = outer // fold
    right = dot_t(wopt_ref[outer:, :], norm)
    for r in range(rows):
        pieces = [
            right[f * groups : (f + 1) * groups, r * seqs : (r + 1) * seqs] * mask
            for f in range(fold)
        ]
        part_ref[r * groups : (r + 1) * groups, :] = jnp.concatenate(pieces, axis=1).astype(BF16)
    left = dot_t(norm, wopt_ref[:outer, :]).astype(BF16)
    for q in range(groups):
        w = jnp.concatenate(
            [wf[pl.ds(f * groups + q, outer, stride=outer), :] for f in range(fold)], axis=1
        ).astype(BF16)
        got = dot(left, w).astype(BF16)
        for f in range(fold):
            for r in range(rows):
                lw_ref[pl.ds((q * fold + f) * seqs, seqs), pl.ds(r * LANES, LANES)] = got[
                    r * seqs : (r + 1) * seqs, f * LANES : (f + 1) * LANES
                ]
    qkvg_ref[...] = dot(norm, wqkvg_ref[...]).astype(BF16)


def pair_kernel(
    dims, pos_s, pos_ref, part_ref, table_ref, wbt_ref, *refs
):
    rows, cols, residues, others, copies = dims
    pair_refs = refs[: others + 1]
    norm_ref, own_ref, msg_ref, table = refs[others + 1 :]
    p = lax.axis_index("pb")
    first = (lax.axis_index("row") * lax.axis_size("br") + lax.axis_index("br")) * rows
    bins = table_ref.shape[0]
    table[...] = jnp.zeros_like(table)
    table[:bins, :] = table_ref[...].astype(F32)
    places = roll_left(pos_ref[...].astype(F32), p * cols)[:1, :]
    at = lax.broadcasted_iota(jnp.int32, (residues, residues), 0)
    to = lax.broadcasted_iota(jnp.int32, (residues, residues), 1)
    column = jnp.sum(jnp.where(at == to, places, 0.0), axis=1, keepdims=True)
    lane = lax.broadcasted_iota(jnp.int32, (residues, LANES), 1).astype(F32)
    tab = table[...].astype(BF16)
    norms = []
    for i in range(rows):
        here = pos_s[first + i].astype(F32)
        bin_of = jnp.clip(here - column, -RELPOS_MAX, RELPOS_MAX) + RELPOS_MAX
        added = dot((lane == bin_of).astype(F32).astype(BF16), tab)
        state = jnp.concatenate([ref[i].astype(F32) for ref in pair_refs], axis=0) + added
        own_ref[i * cols : (i + 1) * cols, :] = state[:cols, :]
        norms.append(normalize(state))
    norm = jnp.concatenate(norms, axis=0)
    norm_ref[...] = norm
    bias = dot_t(wbt_ref[...], norm).astype(BF16)
    heads = wbt_ref.shape[0]
    blocks = bias.shape[1] // LANES
    split = part_ref.shape[0]
    flat = jnp.concatenate(
        [bias[:, b * LANES : (b + 1) * LANES].astype(F32) for b in range(blocks)], axis=0
    ).astype(BF16)
    del heads
    part = part_ref[...]
    for c in range(copies):
        msg_ref[c, :split, :] = part
        msg_ref[c, split:, :] = flat


def column_kernel(
    dims, h_ref, qkvg_ref, gen_ref, wqkvg_ref, wout_ref, wexp_ref, wcon_ref, *refs
):
    seqs, rows, blocks, others = dims
    other_refs = refs[:others]
    out_ref, hs, os = refs[others:]
    p = lax.axis_index("pb")
    width = wout_ref.shape[0]
    scale = SUBSPACE_DEPTH ** (-0.5)
    keys, values = [], []
    for ref in other_refs:
        hs[...] = ref[...].astype(F32)
        norm = jnp.concatenate(
            [normalize(residue_rows(hs, r, seqs, rows, blocks)) for r in range(rows)], axis=0
        )
        kv = dot(norm, wqkvg_ref[:, width : 3 * width]).astype(BF16)
        keys.append(kv[:, :width])
        values.append(kv[:, width:])
    hs[...] = h_ref[...].astype(F32)
    total = seqs * (others + 1)
    bias = (roll_left(gen_ref[...].astype(F32), p * seqs)[:1, :] - 1.0) * MASK_NEGATIVE
    head = lax.broadcasted_iota(jnp.int32, (seqs, width), 1) // SUBSPACE_DEPTH
    ones = jnp.ones((total, LANES), BF16)
    gated = []
    for r in range(rows):
        span = slice(r * seqs, (r + 1) * seqs)
        query = qkvg_ref[span, :width].astype(F32)
        stacked = jnp.concatenate(
            [jnp.where(head == a, query, 0.0).astype(BF16) for a in range(VERTICAL_ATTENDS)], axis=0
        )
        key = jnp.concatenate([qkvg_ref[span, width : 2 * width]] + [k[span] for k in keys], axis=0)
        value = jnp.concatenate(
            [qkvg_ref[span, 2 * width : 3 * width]] + [v[span] for v in values], axis=0
        )
        scores = dot_t(stacked, key) * scale + bias
        top = jnp.max(scores, axis=-1, keepdims=True)
        weights = jnp.exp(scores - top).astype(BF16)
        mixed = dot(weights, value)
        sums = dot(weights, ones)
        sums = jnp.concatenate([sums] * (width // LANES), axis=1)
        num, den = mixed[:seqs], sums[:seqs]
        for a in range(1, VERTICAL_ATTENDS):
            part = slice(a * seqs, (a + 1) * seqs)
            num = jnp.where(head == a, mixed[part], num)
            den = jnp.where(head == a, sums[part], den)
        gate = jax.nn.sigmoid(qkvg_ref[span, 3 * width :].astype(F32))
        gated.append((gate * (num / den)).astype(BF16))
    start = jnp.concatenate(
        [residue_rows(hs, r, seqs, rows, blocks) for r in range(rows)], axis=0
    )
    mid = start + dot(jnp.concatenate(gated, axis=0), wout_ref[...])
    hidden = jnp.maximum(dot(normalize(mid), wexp_ref[...]), 0.0).astype(BF16)
    done = mid + dot(hidden, wcon_ref[...])
    for r in range(rows):
        for b in range(blocks):
            os[pl.ds(b * rows + r, seqs, stride=rows * blocks), :] = done[
                r * seqs : (r + 1) * seqs, b * LANES : (b + 1) * LANES
            ]
    out_ref[...] = os[...].astype(BF16)


def outer_kernel(dims, recv_ref, lw_ref, own_ref, *refs):
    rows, cols, split, others = dims
    send_refs = refs[:others]
    rf, acc = refs[others:]
    sources = recv_ref.shape[0]
    groups = split // rows
    p = lax.axis_index("pb")
    for k in range(sources):
        rf[k * split : (k + 1) * split, :] = recv_ref[k, :split, :].astype(F32)
    got = None
    for q in range(groups):
        part = rf[pl.ds(q, sources * rows, stride=groups), :].astype(BF16)
        term = dot(part, lw_ref[q * LANES : (q + 1) * LANES, :])
        got = term if got is None else got + term
    acc[...] = got
    for d in range(others + 1):
        where = pl.multiple_of(lax.rem(p + d, others + 1) * cols, cols)
        block = acc[pl.ds(where, cols), :]
        for i in range(rows):
            piece = block[:, i * LANES : (i + 1) * LANES]
            if d == 0:
                own_ref[i * cols : (i + 1) * cols, :] = piece
            else:
                send_refs[d - 1][i * cols : (i + 1) * cols, :] = piece.astype(BF16)


def triangle_kernel(
    dims, norm_ref, wtri_ref, recv_ref, res_ref, wto_ref, upd_ref, bs, bh
):
    rows, cols, residues, split = dims
    p = lax.axis_index("pb")
    depth = SUBSPACE_DEPTH
    scale = depth ** (-0.5)
    near = cols // rows
    width = recv_ref.shape[1] - split
    first = p * near
    for a in range(near):
        bs[a * width : (a + 1) * width, :] = recv_ref[first + a, split:, :].astype(F32)
    key_mask = (roll_left(res_ref[...].astype(F32), p * cols)[:1, :] - 1.0) * MASK_NEGATIVE
    biases = []
    for h in range(TRI_HEADS):
        if residues <= LANES:
            fold = LANES // residues
            got = bs[pl.ds(h, cols // fold, stride=TRI_HEADS), :]
            for f in range(fold):
                bh[pl.ds(f, cols // fold, stride=fold), :] = got[
                    :, f * residues : (f + 1) * residues
                ]
        else:
            fold = residues // LANES
            for f in range(fold):
                bh[:, f * LANES : (f + 1) * LANES] = bs[
                    pl.ds(f * TRI_HEADS + h, cols, stride=fold * TRI_HEADS), :
                ]
        biases.append(bh[...] + key_mask)
    proj = dot(norm_ref[...], wtri_ref[...])
    kind = lax.broadcasted_iota(jnp.int32, (1, LANES), 1) // depth
    mixed_rows = []
    for i in range(rows):
        base = i * residues
        total = None
        for h in range(TRI_HEADS):
            block = proj[base : base + residues, h * LANES : (h + 1) * LANES].astype(BF16).astype(F32)
            mine = block[:cols]
            query = jnp.where(kind == 0, mine, 0.0).astype(BF16)
            key = pltpu.roll(block, LANES - depth, 1).astype(BF16)
            scores = dot_t(query, key) * scale + biases[h]
            top = jnp.max(scores, axis=-1, keepdims=True)
            grown = jnp.exp(scores - top)
            sums = jnp.sum(grown, axis=-1, keepdims=True)
            mixed = dot(grown.astype(BF16), block.astype(BF16)) / sums
            gate = jax.nn.sigmoid(pltpu.roll(mine, LANES - depth, 1))
            out = jnp.where(kind == 2, gate * mixed, 0.0)
            out = pltpu.roll(out, (h * depth - 2 * depth) % LANES, 1) if h != 2 else out
            total = out if total is None else total + out
        mixed_rows.append(total)
    upd_ref[...] = dot(jnp.concatenate(mixed_rows, axis=0).astype(BF16), wto_ref[...])


def final_kernel(dims, gen_ref, in_ref, upd_ref, own_ref, up_ref, down_ref, *refs):
    others = dims
    recv_refs = refs[:others]
    (out_ref,) = refs[others:]
    count = jnp.sum(gen_ref[...].astype(F32), axis=1, keepdims=True)
    outer = own_ref[...]
    for ref in recv_refs:
        outer = outer + ref[...].astype(F32)
    mid = in_ref[...] + upd_ref[...] + outer / count
    hidden = jnp.maximum(dot(normalize(mid), up_ref[...]), 0.0).astype(BF16)
    out_ref[...] = (mid + dot(hidden, down_ref[...])).astype(BF16)


def on_device(
    homolog_representation,
    pair_state,
    genuine_chain_indicator,
    resolved_mask,
    crop_positions,
    relative_position_table,
    column_query_key_value_gate,
    vertical_attention_projector,
    expansion_coefficients,
    contraction_coefficients,
    operand_duo_projector,
    tensor_product_projector,
    triangle_query_key_value_gate,
    triangle_bias_weight,
    triangle_output_weight,
    pair_up_weight,
    pair_down_weight,
):
    seqs, rows, width = homolog_representation.shape
    cols, channels = pair_state.shape[1:]
    residues = resolved_mask.shape[0]
    parts = lax.axis_size("pb")
    others = parts - 1
    copies = lax.axis_size("row") * lax.axis_size("br")
    blocks = width // LANES
    outer = operand_duo_projector.shape[1] // 2
    fold = LANES // seqs
    groups = outer // fold
    split = rows * groups
    sds = jax.ShapeDtypeStruct

    def from_ahead(x, d):
        return lax.ppermute(x, "pb", [(n, (n - d) % parts) for n in range(parts)])

    pair_others = [from_ahead(pair_state, d) for d in range(1, parts)]
    flat = (
        homolog_representation.reshape(seqs, rows, blocks, LANES)
        .transpose(0, 2, 1, 3)
        .reshape(seqs * blocks * rows, LANES)
    )
    flat_others = [from_ahead(flat, d) for d in range(1, parts)]
    gen = genuine_chain_indicator.reshape(1, -1)
    res = resolved_mask.reshape(1, -1)
    pos = crop_positions.reshape(1, -1)

    qkvg, part, lw = call(
        functools.partial(local_kernel, (seqs, rows, blocks, outer)),
        (
            sds((seqs * rows, 4 * width), BF16),
            sds((split, LANES), BF16),
            sds((outer * seqs, rows * LANES), BF16),
        ),
        (flat, column_query_key_value_gate, operand_duo_projector.T, tensor_product_projector, gen),
        scratch=[
            pltpu.VMEM((seqs * blocks * rows, LANES), F32),
            pltpu.VMEM((outer * outer, LANES), F32),
        ],
        flops=3 * 10**9,
        name="local",
    )
    tail = rows * residues * TRI_HEADS // LANES
    norm, pair_own, msg = call(
        functools.partial(pair_kernel, (rows, cols, residues, others, copies)),
        (
            sds((rows * residues, channels), BF16),
            sds((rows * cols, channels), F32),
            sds((copies, split + tail, LANES), BF16),
        ),
        (
            crop_positions, pos, part, relative_position_table, triangle_bias_weight.T,
            pair_state, *pair_others,
        ),
        smem=(0,),
        scratch=[pltpu.VMEM((LANES, channels), F32)],
        flops=10**9,
        name="pair",
    )
    recv = lax.all_to_all(msg, ("row", "br"), 0, 0, tiled=True)
    refreshed = call(
        functools.partial(column_kernel, (seqs, rows, blocks, others)),
        sds((seqs * blocks * rows, LANES), BF16),
        (
            flat, qkvg, gen, column_query_key_value_gate, vertical_attention_projector,
            expansion_coefficients, contraction_coefficients, *flat_others,
        ),
        scratch=[pltpu.VMEM((seqs * blocks * rows, LANES), F32)] * 2,
        flops=6 * 10**9,
        name="column",
    )
    opm = call(
        functools.partial(outer_kernel, (rows, cols, split, others)),
        (sds((rows * cols, channels), F32),) + (sds((rows * cols, channels), BF16),) * others,
        (recv, lw),
        scratch=[
            pltpu.VMEM((copies * split, LANES), F32),
            pltpu.VMEM((residues, rows * channels), F32),
        ],
        flops=10**9,
        name="outer",
    )
    opm_others = [from_behind(opm[d], d, parts) for d in range(1, parts)]
    update = call(
        functools.partial(triangle_kernel, (rows, cols, residues, split)),
        sds((rows * cols, channels), F32),
        (norm, triangle_query_key_value_gate, recv, res, triangle_output_weight),
        scratch=[
            pltpu.VMEM((cols // rows * tail, LANES), F32),
            pltpu.VMEM((cols, residues), F32),
        ],
        flops=2 * 10**9,
        name="triangle",
    )
    pair_updated = call(
        functools.partial(final_kernel, others),
        sds((rows * cols, channels), BF16),
        (gen, pair_own, update, opm[0], pair_up_weight, pair_down_weight, *opm_others),
        flops=10**9,
        name="final",
    )
    return (
        refreshed.reshape(seqs, blocks, rows, LANES).transpose(0, 2, 1, 3).reshape(seqs, rows, width),
        pair_updated.reshape(rows, cols, channels),
    )


def from_behind(x, d, parts):
    return lax.ppermute(x, "pb", [(n, (n + d) % parts) for n in range(parts)])


def solution(mesh):
    msa = P(("grp", "pb"), ("row", "br"), None)
    pair = P(("grp", "row", "br"), "pb", None)
    return jax.shard_map(
        on_device,
        mesh=mesh,
        in_specs=(msa, pair, P("grp"), P("grp"), P("grp")) + (P(),) * 12,
        out_specs=(msa, pair),
        check_vma=False,
    )
```

```python
import functools
import math

import jax
import jax.numpy as jnp
from jax import lax
from jax.experimental import pallas as pl
from jax.experimental.pallas import tpu as pltpu
from jax.sharding import PartitionSpec as P

VERTICAL_ATTENDS = 8
TRI_HEADS = 4
SUBSPACE_DEPTH = 32
RELPOS_MAX = 32
NORM_EPS = 1e-05
MASK_NEGATIVE = 1000000000.0
LANES = 128
F32 = jnp.float32
BF16 = jnp.bfloat16


def normalize(values):
    centre = jnp.mean(values, axis=-1, keepdims=True)
    centred = values - centre
    spread = jnp.mean(centred * centred, axis=-1, keepdims=True)
    return (centred * lax.rsqrt(spread + NORM_EPS)).astype(BF16)


def dot(a, b):
    return jnp.dot(a, b, preferred_element_type=F32)


def dot_t(a, b):
    return lax.dot_general(a, b, (((1,), (1,)), ((), ())), preferred_element_type=F32)


def residue_rows(scratch, residue, seqs, rows, blocks):
    step = rows * blocks
    parts = [scratch[pl.ds(b * rows + residue, seqs, stride=step), :] for b in range(blocks)]
    return jnp.concatenate(parts, axis=1)


def roll_left(row, amount):
    n = row.shape[1]
    wide = jnp.broadcast_to(row, (8, n))
    return pltpu.roll(wide, lax.rem(n - amount, n), 1)


def partner(here, d, n):
    return here ^ d if n & (n - 1) == 0 else (here + d) % n


def call(body, out_shape, args, anywhere=(), scratch=(), flops=10**8, name=None, limit=16 << 20):
    specs = [
        pl.BlockSpec(memory_space=pltpu.HBM if n in anywhere else pltpu.VMEM)
        for n in range(len(args))
    ]
    outs = jax.tree.map(lambda _: pl.BlockSpec(memory_space=pltpu.VMEM), out_shape)
    return pl.pallas_call(
        body,
        out_shape=out_shape,
        in_specs=specs,
        out_specs=outs,
        scratch_shapes=list(scratch),
        name=name,
        compiler_params=pltpu.CompilerParams(vmem_limit_bytes=limit),
        cost_estimate=pl.CostEstimate(flops=flops, bytes_accessed=1 << 20, transcendentals=0),
    )(*args)


def lane_blocks(rows):
    parts = [rows[:, b * LANES : (b + 1) * LANES] for b in range(rows.shape[1] // LANES)]
    short = -len(parts) * rows.shape[0] % 8
    if short:
        parts.append(jnp.zeros((short, LANES), rows.dtype))
    return jnp.concatenate(parts, axis=0)


def early_kernel(dims, *refs):
    seqs, rows, blocks, outer, cols, residues = dims
    count = 7
    sources, refs = refs[:count], refs[count:]
    msg_ref, left_ref, norm_ref, added_ref, own_ref, pnorm_ref, *scratch = refs
    bufs, (hs, table, sems) = scratch[:count], scratch[count:]
    copies = [pltpu.make_async_copy(x, y, sems.at[n]) for n, (x, y) in enumerate(zip(sources, bufs))]
    for copy in copies:
        copy.start()
    h_ref, wopt_ref, gen_ref, pos_ref, table_ref, pair_ref, wbt_ref = bufs
    p = lax.axis_index("pb")
    first = (lax.axis_index("row") * lax.axis_size("br") + lax.axis_index("br")) * rows
    for copy in copies:
        copy.wait()
    spots = pos_ref[...].astype(F32)
    places = roll_left(spots, p * cols)[:1, :]
    at = lax.broadcasted_iota(jnp.int32, (residues, residues), 0)
    to = lax.broadcasted_iota(jnp.int32, (residues, residues), 1)
    column = jnp.sum(jnp.where(at == to, places, 0.0), axis=1, keepdims=True)
    lane = lax.broadcasted_iota(jnp.int32, (residues, LANES), 1).astype(F32)
    slot = lax.broadcasted_iota(jnp.int32, (1, residues), 1)
    bins = table_ref.shape[0]
    table[...] = jnp.zeros_like(table)
    table[:bins, :] = table_ref[...].astype(F32)
    tab = table[...].astype(BF16)
    pairs = []
    for i in range(rows):
        here = jnp.sum(jnp.where(slot == first + i, spots, 0.0), axis=1, keepdims=True)
        bin_of = jnp.clip(here - column, -RELPOS_MAX, RELPOS_MAX) + RELPOS_MAX
        got = dot((lane == bin_of).astype(F32).astype(BF16), tab)
        state = got[:cols] + pair_ref[i].astype(F32)
        own_ref[i * cols : (i + 1) * cols, :] = state
        added_ref[i] = got[cols:]
        pairs.append(normalize(state))
    pairs = jnp.concatenate(pairs, axis=0)
    pnorm_ref[...] = pairs
    hs[...] = h_ref[...].astype(F32)
    norm = jnp.concatenate(
        [normalize(residue_rows(hs, r, seqs, rows, blocks)) for r in range(rows)], axis=0
    )
    norm_ref[...] = norm
    mask = roll_left(gen_ref[...].astype(F32), p * seqs)[:1, :seqs]
    fold = LANES // seqs
    groups = outer // fold
    right = dot_t(wopt_ref[outer:, :], norm)
    for r in range(rows):
        pieces = [
            right[f * groups : (f + 1) * groups, r * seqs : (r + 1) * seqs] * mask
            for f in range(fold)
        ]
        msg_ref[r * groups : (r + 1) * groups, :] = jnp.concatenate(pieces, axis=1).astype(BF16)
    msg_ref[rows * groups :, :] = lane_blocks(dot_t(wbt_ref[...], pairs)).astype(BF16)
    left_ref[...] = dot_t(norm, wopt_ref[:outer, :]).astype(BF16)


def project_kernel(dims, norm_ref, left_ref, wqkvg_ref, wtp_ref, qkvg_ref, lw_ref, wf):
    seqs, rows, outer = dims
    fold = LANES // seqs
    groups = outer // fold
    wf[...] = wtp_ref[...].astype(F32)
    qkvg_ref[...] = dot(norm_ref[...], wqkvg_ref[...]).astype(BF16)
    left = left_ref[...]
    for q in range(groups):
        w = jnp.concatenate(
            [wf[pl.ds(f * groups + q, outer, stride=outer), :] for f in range(fold)], axis=1
        ).astype(BF16)
        got = dot(left, w).astype(BF16)
        for f in range(fold):
            for r in range(rows):
                lw_ref[pl.ds((q * fold + f) * seqs, seqs), pl.ds(r * LANES, LANES)] = got[
                    r * seqs : (r + 1) * seqs, f * LANES : (f + 1) * LANES
                ]


def gather_kernel(low, *refs):
    out_ref = refs[-1]
    here = (lax.axis_index("row") * lax.axis_size("br") + lax.axis_index("br")) // low
    for d, ref in enumerate(refs[:-1]):
        out_ref[partner(here, d, len(refs) - 1)] = ref[...]


def column_kernel(dims, qkvg_ref, gen_ref, wqkvg_ref, *refs):
    seqs, rows, blocks, others = dims
    other_refs = refs[:others]
    out_ref, hs = refs[others:]
    p = lax.axis_index("pb")
    width = wqkvg_ref.shape[0]
    scale = SUBSPACE_DEPTH ** (-0.5)
    keys, values = [], []
    for ref in other_refs:
        hs[...] = ref[...].astype(F32)
        norm = jnp.concatenate(
            [normalize(residue_rows(hs, r, seqs, rows, blocks)) for r in range(rows)], axis=0
        )
        kv = dot(norm, wqkvg_ref[:, width : 3 * width]).astype(BF16)
        keys.append(kv[:, :width])
        values.append(kv[:, width:])
    total = seqs * (others + 1)
    bias = (roll_left(gen_ref[...].astype(F32), p * seqs)[:1, :] - 1.0) * MASK_NEGATIVE
    head = lax.broadcasted_iota(jnp.int32, (1, width), 1) // SUBSPACE_DEPTH
    picks = [(head == a).astype(F32).astype(BF16) for a in range(VERTICAL_ATTENDS)]
    ones = jnp.concatenate([jnp.broadcast_to(m, (total, width)) for m in picks], axis=0)
    for r in range(rows):
        span = slice(r * seqs, (r + 1) * seqs)
        query = qkvg_ref[span, :width]
        stacked = jnp.concatenate([query * m for m in picks], axis=0)
        key = jnp.concatenate([qkvg_ref[span, width : 2 * width]] + [k[span] for k in keys], axis=0)
        value = jnp.concatenate(
            [qkvg_ref[span, 2 * width : 3 * width]] + [v[span] for v in values], axis=0
        )
        scores = dot_t(stacked, key) * scale + bias
        top = jnp.max(scores, axis=-1, keepdims=True)
        weights = jnp.exp(scores - top).astype(BF16)
        wide = jnp.concatenate(
            [weights[a * seqs : (a + 1) * seqs] for a in range(VERTICAL_ATTENDS)], axis=1
        )
        num = dot(wide, jnp.concatenate([value * m for m in picks], axis=0))
        den = dot(wide, ones)
        gate = jax.nn.sigmoid(qkvg_ref[span, 3 * width :].astype(F32))
        out_ref[span, :] = (gate * (num / den)).astype(BF16)


def transition_kernel(dims, h_ref, gated_ref, wout_ref, wexp_ref, wcon_ref, out_ref, hs, os):
    seqs, rows, blocks = dims
    hs[...] = h_ref[...].astype(F32)
    start = jnp.concatenate(
        [residue_rows(hs, r, seqs, rows, blocks) for r in range(rows)], axis=0
    )
    mid = start + dot(gated_ref[...], wout_ref[...])
    hidden = jnp.maximum(dot(normalize(mid), wexp_ref[...]), 0.0).astype(BF16)
    done = mid + dot(hidden, wcon_ref[...])
    for r in range(rows):
        for b in range(blocks):
            os[pl.ds(b * rows + r, seqs, stride=rows * blocks), :] = done[
                r * seqs : (r + 1) * seqs, b * LANES : (b + 1) * LANES
            ]
    out_ref[...] = os[...].astype(BF16)


def outer_kernel(dims, lw_ref, *refs):
    rows, cols, split, others, low = dims
    recv_refs, refs = refs[:low], refs[low:]
    own_ref, bias_ref, send_refs = refs[0], refs[1], refs[2 : 2 + others]
    rf, bs, acc = refs[2 + others :]
    high = recv_refs[0].shape[0]
    groups = split // rows
    width = bs.shape[0] // (high * low)
    p = lax.axis_index("pb")
    here = (lax.axis_index("row") * lax.axis_size("br") + lax.axis_index("br")) % low
    for e in range(low):
        place = partner(here, e, low)
        for k in range(high):
            where = pl.multiple_of((k * low + place) * split, split)
            rf[pl.ds(where, split), :] = recv_refs[e][k, :split, :].astype(F32)
            bs[pl.ds((k * low + place) * width, width), :] = recv_refs[e][
                k, split : split + width, :
            ].astype(F32)
    got = None
    for q in range(groups):
        part = rf[pl.ds(q, high * low * rows, stride=groups), :].astype(BF16)
        term = dot(part, lw_ref[q * LANES : (q + 1) * LANES, :])
        got = term if got is None else got + term
    acc[...] = got
    count = rows * cols
    near = cols // rows * width
    for d in range(others + 1):
        there = lax.rem(p + d, others + 1)
        block = acc[pl.ds(pl.multiple_of(there * cols, cols), cols), :]
        bias = bs[pl.ds(pl.multiple_of(there * near, near), near), :]
        for i in range(rows):
            piece = block[:, i * LANES : (i + 1) * LANES]
            if d == 0:
                own_ref[i * cols : (i + 1) * cols, :] = piece
            else:
                send_refs[d - 1][i * cols : (i + 1) * cols, :] = piece.astype(BF16)
        if d == 0:
            bias_ref[...] = bias
        else:
            send_refs[d - 1][count:, :] = bias.astype(BF16)


def scores_kernel(dims, pnorm_ref, added_ref, wtri_ref, *refs):
    rows, cols, residues, others = dims
    pair_refs = refs[:others]
    scores_ref, value_ref, gate_ref = refs[others:]
    depth = SUBSPACE_DEPTH
    scale = depth ** (-0.5)
    kind = lax.broadcasted_iota(jnp.int32, (1, LANES), 1) // depth
    picks = [(kind == h).astype(F32).astype(BF16) for h in range(TRI_HEADS)]
    weight = wtri_ref[...].astype(F32)
    sorted_by_kind = []
    for t in range(4):
        total = None
        for h in range(TRI_HEADS):
            block = jnp.where(kind == t, weight[:, h * LANES : (h + 1) * LANES], 0.0)
            shift = ((h - t) * depth) % LANES
            block = pltpu.roll(block, shift, 1) if shift else block
            total = block if total is None else total + block
        sorted_by_kind.append(total.astype(BF16))
    mine = pnorm_ref[...]
    parts = []
    for i in range(rows):
        parts.append(mine[i * cols : (i + 1) * cols])
        for d in range(others):
            state = pair_refs[d][i].astype(F32) + added_ref[i, d * cols : (d + 1) * cols, :]
            parts.append(normalize(state))
    norm = jnp.concatenate(parts, axis=0)
    both = dot(norm, jnp.concatenate(sorted_by_kind[1:3], axis=1)).astype(BF16)
    value_ref[...] = both[:, LANES:]
    asked = dot(mine, jnp.concatenate([sorted_by_kind[0], sorted_by_kind[3]], axis=1)).astype(BF16)
    gate_ref[...] = jax.nn.sigmoid(asked[:, LANES:].astype(F32))
    for i in range(rows):
        query = asked[i * cols : (i + 1) * cols, :LANES]
        stacked = jnp.concatenate([query * m for m in picks], axis=0)
        key = both[i * residues : (i + 1) * residues, :LANES]
        scores_ref[i] = dot_t(stacked, key) * scale


def final_kernel(
    dims, gen_ref, res_ref, in_ref, scores_ref, value_ref, gate_ref, own_ref, bias_ref,
    wto_ref, up_ref, down_ref, *refs,
):
    rows, cols, residues, others = dims
    recv_refs = refs[:others]
    out_ref, bs, bh = refs[others:]
    p = lax.axis_index("pb")
    count = rows * cols
    near = bias_ref.shape[0]
    width = near * rows // cols
    for d in range(others + 1):
        bs[...] = bias_ref[...] if d == 0 else recv_refs[d - 1][count:, :].astype(F32)
        base = d * TRI_HEADS * cols
        for h in range(TRI_HEADS):
            for i in range(rows):
                block, at = divmod(i * cols, LANES)
                got = bs[pl.ds(block * TRI_HEADS + h, cols // rows, stride=width), :]
                bh[pl.ds(base + h * cols + i, cols // rows, stride=rows), :] = got[:, at : at + cols]
    key_mask = (roll_left(res_ref[...].astype(F32), p * cols)[:1, :] - 1.0) * MASK_NEGATIVE
    size = TRI_HEADS * cols
    bias = jnp.concatenate([bh[d * size : (d + 1) * size, :] for d in range(others + 1)], axis=1)
    bias = bias + key_mask
    kind = lax.broadcasted_iota(jnp.int32, (cols, LANES), 1) // SUBSPACE_DEPTH
    mixed_rows = []
    for i in range(rows):
        scores = scores_ref[i] + bias
        top = jnp.max(scores, axis=-1, keepdims=True)
        grown = jnp.exp(scores - top)
        sums = jnp.sum(grown, axis=-1, keepdims=True)
        mixed = dot(grown.astype(BF16), value_ref[i * residues : (i + 1) * residues, :]) / sums
        total = mixed[:cols]
        for h in range(1, TRI_HEADS):
            total = jnp.where(kind == h, mixed[h * cols : (h + 1) * cols], total)
        mixed_rows.append(total)
    gated = (gate_ref[...] * jnp.concatenate(mixed_rows, axis=0)).astype(BF16)
    update = dot(gated, wto_ref[...])
    total = jnp.sum(gen_ref[...].astype(F32), axis=1, keepdims=True)
    outer = own_ref[...]
    for ref in recv_refs:
        outer = outer + ref[:count, :].astype(F32)
    mid = in_ref[...] + update + outer / total
    hidden = jnp.maximum(dot(normalize(mid), up_ref[...]), 0.0).astype(BF16)
    out_ref[...] = (mid + dot(hidden, down_ref[...])).astype(BF16)


def on_device(
    homolog_representation,
    pair_state,
    genuine_chain_indicator,
    resolved_mask,
    crop_positions,
    relative_position_table,
    column_query_key_value_gate,
    vertical_attention_projector,
    expansion_coefficients,
    contraction_coefficients,
    operand_duo_projector,
    tensor_product_projector,
    triangle_query_key_value_gate,
    triangle_bias_weight,
    triangle_output_weight,
    pair_up_weight,
    pair_down_weight,
):
    seqs, rows, width = homolog_representation.shape
    cols, channels = pair_state.shape[1:]
    residues = resolved_mask.shape[0]
    parts = lax.axis_size("pb")
    others = parts - 1
    copies = lax.axis_size("row") * lax.axis_size("br")
    blocks = width // LANES
    outer = operand_duo_projector.shape[1] // 2
    fold = LANES // seqs
    groups = outer // fold
    split = rows * groups
    sds = jax.ShapeDtypeStruct

    low = math.gcd(copies, 4)
    high = copies // low

    def from_ahead(x, d):
        return lax.ppermute(x, "pb", [(n, (n - d) % parts) for n in range(parts)])

    def from_high(x, d):
        pairs = [(n, partner(n // low, d, high) * low + n % low) for n in range(copies)]
        return lax.ppermute(x, ("row", "br"), pairs)

    def from_low(x, d):
        pairs = [(n, n // low * low + partner(n % low, d, low)) for n in range(copies)]
        return lax.ppermute(x, ("row", "br"), pairs)

    flat = (
        homolog_representation.reshape(seqs, rows, blocks, LANES)
        .transpose(0, 2, 1, 3)
        .reshape(seqs * blocks * rows, LANES)
    )
    gen = genuine_chain_indicator.reshape(1, -1)
    res = resolved_mask.reshape(1, -1)
    pos = crop_positions.reshape(1, -1)
    table = relative_position_table
    wopt = operand_duo_projector.T
    wbt = triangle_bias_weight.T
    flat_shape = (seqs * blocks * rows, LANES)
    width_b = rows * cols * TRI_HEADS // LANES
    tail = -(-width_b // 8) * 8
    inputs = (flat, wopt, gen, pos, table, pair_state, wbt)

    msg, left, hnorm, added, pair_own, pnorm = call(
        functools.partial(early_kernel, (seqs, rows, blocks, outer, cols, residues)),
        (
            sds((split + tail, LANES), BF16),
            sds((rows * seqs, outer), BF16),
            sds((rows * seqs, width), BF16),
            sds((rows, residues - cols, channels), F32),
            sds((rows * cols, channels), F32),
            sds((rows * cols, channels), BF16),
        ),
        tuple(pltpu.with_memory_space_constraint(x, pltpu.HBM) for x in inputs),
        anywhere=range(len(inputs)),
        scratch=[pltpu.VMEM(x.shape, x.dtype) for x in inputs]
        + [
            pltpu.VMEM(flat_shape, F32),
            pltpu.VMEM((LANES, channels), F32),
            pltpu.SemaphoreType.DMA((len(inputs),)),
        ],
        flops=10**9,
        name="early",
    )
    near = [from_high(msg, d) for d in range(1, high)]
    pair_late, flat_late, _ = lax.optimization_barrier((pair_state, flat, msg))
    pair_others = [from_ahead(pair_late, d) for d in range(1, parts)]
    flat_others = [from_ahead(flat_late, d) for d in range(1, parts)]
    qkvg, lw = call(
        functools.partial(project_kernel, (seqs, rows, outer)),
        (sds((seqs * rows, 4 * width), BF16), sds((outer * seqs, rows * LANES), BF16)),
        (hnorm, left, column_query_key_value_gate, tensor_product_projector),
        scratch=[pltpu.VMEM((outer * outer, LANES), F32)],
        flops=2 * 10**9,
        name="project",
    )
    *near, qkvg, lw = lax.optimization_barrier((*near, qkvg, lw))
    block = call(
        functools.partial(gather_kernel, low),
        sds((high, split + tail, LANES), BF16),
        (msg, *near),
        flops=10**6,
        name="gather",
    )
    block, qkvg, pnorm = lax.optimization_barrier((block, qkvg, pnorm))
    recv = [from_low(block, d) for d in range(1, low)]
    scores, value, gate = call(
        functools.partial(scores_kernel, (rows, cols, residues, others)),
        (
            sds((rows, TRI_HEADS * cols, residues), F32),
            sds((rows * residues, channels), BF16),
            sds((rows * cols, channels), F32),
        ),
        (pnorm, added, triangle_query_key_value_gate, *pair_others),
        flops=2 * 10**9,
        name="scores",
    )
    gated = call(
        functools.partial(column_kernel, (seqs, rows, blocks, others)),
        sds((seqs * rows, width), BF16),
        (qkvg, gen, column_query_key_value_gate, *flat_others),
        scratch=[pltpu.VMEM(flat_shape, F32)],
        flops=4 * 10**9,
        name="column",
    )
    *recv, scores, value, gate, gated = lax.optimization_barrier(
        (*recv, scores, value, gate, gated)
    )
    recv = [block] + recv
    near_rows = cols // rows * width_b
    own, bias, *send = call(
        functools.partial(outer_kernel, (rows, cols, split, others, low)),
        (sds((rows * cols, channels), F32), sds((near_rows, LANES), F32))
        + (sds((rows * cols + near_rows, channels), BF16),) * others,
        (lw, *recv),
        scratch=[
            pltpu.VMEM((copies * split, LANES), F32),
            pltpu.VMEM((copies * width_b, LANES), F32),
            pltpu.VMEM((residues, rows * channels), F32),
        ],
        flops=10**9,
        name="outer",
    )
    send = list(send)
    *send, gated = lax.optimization_barrier((*send, gated))
    got = [from_behind(send[d - 1], d, parts) for d in range(1, parts)]
    refreshed = call(
        functools.partial(transition_kernel, (seqs, rows, blocks)),
        sds(flat_shape, BF16),
        (
            flat, gated, vertical_attention_projector,
            expansion_coefficients, contraction_coefficients,
        ),
        scratch=[pltpu.VMEM(flat_shape, F32)] * 2,
        flops=4 * 10**9,
        name="transition",
    )
    *got, refreshed = lax.optimization_barrier((*got, refreshed))
    pair_updated = call(
        functools.partial(final_kernel, (rows, cols, residues, others)),
        sds((rows * cols, channels), BF16),
        (
            gen, res, pair_own, scores, value, gate, own, bias,
            triangle_output_weight, pair_up_weight, pair_down_weight, *got,
        ),
        scratch=[
            pltpu.VMEM((near_rows, LANES), F32),
            pltpu.VMEM((TRI_HEADS * residues, cols), F32),
        ],
        flops=10**9,
        name="final",
    )
    return (
        refreshed.reshape(seqs, blocks, rows, LANES).transpose(0, 2, 1, 3).reshape(seqs, rows, width),
        pair_updated.reshape(rows, cols, channels),
    )


def from_behind(x, d, parts):
    return lax.ppermute(x, "pb", [(n, (n + d) % parts) for n in range(parts)])


def solution(mesh):
    msa = P(("grp", "pb"), ("row", "br"), None)
    pair = P(("grp", "row", "br"), "pb", None)
    return jax.shard_map(
        on_device,
        mesh=mesh,
        in_specs=(msa, pair, P("grp"), P("grp"), P("grp")) + (P(),) * 12,
        out_specs=(msa, pair),
        check_vma=False,
    )
```
